128 devices in a mesh: wl: 32 (over x, y, core), tile: 4 (over z).
Axes of the slice: x: 4, y: 4, z: 4, core: 2. Of those that a mesh axis runs over, the one named last changes fastest.
Arguments:
- forward: float32 [128, 2, 1024, 1024], P(('wl', 'tile')), may hold values from -6 to 6
- adjoint: float32 [128, 2, 1024, 1024], P(('wl', 'tile')), may hold values from -6 to 6
- mode: float32 [2, 1024], replicated, may hold values from -6 to 6
- target: float32 [128], P(('wl', 'tile')), may hold values from 0 to 2
- wl_index: int32 [128], P(('wl', 'tile')), may hold values from 0 to 127, each once
- tile_of: int32 [128], replicated, may hold values from 0 to 127, each once
- density: float32 [1024, 1024], P(('wl', 'tile')), may hold values from 0 to 1
Outputs:
- gradient: float32 [1024, 1024], P(('wl', 'tile'))
The draws below stay inside these ranges and needn't reach their ends.
All inputs are finite; a program needn't handle non-finite values.
Results may differ from the reference program's by a relative error of at most 0.00002.
Values sent between devices are 32-bit elements; how exact they have to be, the bound alone decides.
No kernel may reach another device: no remote copies, remote signals or barrier semaphores. Data moves between devices by JAX's collectives and lax.ppermute only.
A program may use at most 64 MiB of HBM per device.

```python
import jax
import jax.numpy as jnp
from jax import lax

ROWS = 1024
COLS = 1024
NWL = 128
N_WL = 32
N_TILE = 4
DEVICES = 128


def block_scale(key, shape, cuts, least, high):
    def one(dim, shards_of):
        steps = jax.random.uniform(jax.random.fold_in(jax.random.fold_in(key, 6), dim), (shards_of,), jnp.float32, least / len(cuts), high / len(cuts))
        return jnp.repeat(jnp.exp(steps), shape[dim] // shards_of).reshape((-1,) + (1,) * (len(shape) - dim - 1))

    loudness = one(*cuts[0])
    for cut in cuts[1:]:
        loudness = loudness * one(*cut)
    return loudness


def bell_draw(own_key, dims, spread, most, shards=(), kind=jnp.bfloat16):
    loudness = block_scale(own_key, dims, shards, -0.22, 0.18) if shards else 1.0
    result = jax.random.normal(own_key, dims, jnp.float32) * spread * loudness
    return jnp.minimum(jnp.maximum(result, -most), most).astype(kind)


def setup_inputs(seed: int = 0) -> dict:
    key_list = jax.random.split(jax.random.key(seed), 8)
    return {
        "forward": bell_draw(key_list[0], (NWL, 2, ROWS, COLS), 1.0, 6.0, ((0, 128),), jnp.float32),
        "adjoint": bell_draw(key_list[1], (NWL, 2, ROWS, COLS), 1.0, 6.0, ((0, 128),), jnp.float32),
        "mode": bell_draw(key_list[2], (2, COLS), 1.0, 6.0, (), jnp.float32),
        "target": jnp.clip(2.0 * jax.random.uniform(key_list[3], (NWL,), jnp.float32) ** block_scale(key_list[3], (NWL,), ((0, 128),), -0.2, 0.2), 0.0, 2.0),
        "wl_index": jax.random.permutation(key_list[4], NWL).astype(jnp.int32),
        "tile_of": jax.random.permutation(key_list[5], DEVICES).astype(jnp.int32),
        "density": jnp.clip(1.0 * jax.random.uniform(key_list[6], (ROWS, COLS), jnp.float32) ** block_scale(key_list[6], (ROWS, COLS), ((0, 128),), -0.2, 0.2), 0.0, 1.0),
    }


def reference(forward, adjoint, mode, target, wl_index, tile_of, density):
    devices = N_WL * N_TILE
    mon = ROWS // 2
    line = forward[:, :, mon, :]
    over_re = lax.optimization_barrier(jnp.sum(line[:, 0] * mode[0] - line[:, 1] * mode[1], axis=1))
    over_im = lax.optimization_barrier(jnp.sum(line[:, 0] * mode[1] + line[:, 1] * mode[0], axis=1))
    fom = (over_re * over_re + over_im * over_im) / COLS
    scale = jnp.sum(fom) / NWL + 1.0
    weight = target - fom / scale
    freq = 1.0 + wl_index.astype(jnp.float32) / NWL

    def accumulate(total, items):
        fwd, adj, wgt, frq = items
        field = frq * frq * (fwd[0] * adj[0] - fwd[1] * adj[1])
        return (total + wgt * field, None)
    start = jnp.zeros((ROWS, COLS), jnp.float32)
    total, _ = lax.scan(accumulate, start, (forward, adjoint, weight, freq))
    tile_rows = ROWS // devices
    arranged = total.reshape(devices, tile_rows, COLS)[tile_of].reshape(ROWS, COLS)
    slope = 4.0 * (1.0 - jnp.tanh(4.0 * (density - 0.5)) ** 2)
    shaped = arranged * slope
    return shaped / jnp.sqrt(jnp.mean(shaped * shaped) + 1e-06)
```

```python
import functools

import jax
import jax.numpy as jnp
from jax import lax
from jax.experimental import pallas as pl
from jax.experimental.pallas import tpu as pltpu
from jax.sharding import Mesh
from jax.sharding import PartitionSpec as P

AXES = ("x", "y", "c", "z")
PLACES = ("x", "y", "z")
SIDE = 4
DEVICES = 128
STRIDE = {"x": 32, "y": 8, "z": 1}
CORE = 4
ROWS = 1024
COLS = 1024
TILE = 8
CUBE = 8
HALF = DEVICES // 2
CHUNK = 8
LANES = 128
MIB = 1 << 20

EVEN = ((0, 1), (2, 3))
ODD = ((0, 3), (1, 2))
FIRST = (EVEN, ODD)
SECOND = (ODD, EVEN)


def cubes(pairs_of_core):
    groups = []
    for core, pairs in enumerate(pairs_of_core):
        for px in pairs:
            for py in pairs:
                for pz in pairs:
                    groups.append(
                        [
                            STRIDE["x"] * x + STRIDE["y"] * y + CORE * core + z
                            for x in px
                            for y in py
                            for z in pz
                        ]
                    )
    return groups


def pair_member(place, odd, bit):
    if odd:
        low = jnp.minimum(place, SIDE - 1 - place)
        return (SIDE - 1 - low) if bit else low
    return (place // 2) * 2 + bit


def owner_parts(core):
    parts = {}
    for axis in PLACES:
        place = lax.axis_index(axis)
        table = []
        for k in (0, 1):
            for j in (0, 1):
                even_first = pair_member(pair_member(place, False, k), True, j)
                odd_first = pair_member(pair_member(place, True, k), False, j)
                chosen = jnp.where(core == 0, even_first, odd_first)
                table.append(chosen * STRIDE[axis])
        parts[axis] = table
    return parts


def flat_index():
    place = CORE * lax.axis_index("c")
    for axis in PLACES:
        place = place + STRIDE[axis] * lax.axis_index(axis)
    return place


def fom_kernel(target, forward, mode, sent, line, sem):
    rows = forward.at[0, :, pl.ds(ROWS // 2, TILE), :]
    copy = pltpu.make_async_copy(rows, line, sem)
    copy.start()
    copy.wait()
    re, im = line[0, 0:1, :], line[1, 0:1, :]
    mode_re, mode_im = mode[0:1, :], mode[1:2, :]
    over_re = jnp.sum(re * mode_re - im * mode_im, axis=1, keepdims=True)
    over_im = jnp.sum(re * mode_im + im * mode_re, axis=1, keepdims=True)
    fom = (over_re * over_re + over_im * over_im) / COLS
    lane = lax.broadcasted_iota(jnp.int32, (1, LANES), 1)
    row = jnp.where(lane < LANES // 2, fom, target[0])
    sent[...] = jnp.broadcast_to(row[None], sent.shape)


def field_kernel(away, tile_of, wl_index, forward, adjoint, out, fwd, adj, sems):
    core = lax.axis_index("c")
    keeper = (1 - core) if away else core
    parts = owner_parts(keeper)

    def owner(block):
        k, j = divmod(block, CUBE)
        total = CORE * keeper
        for shift, axis in zip((2, 1, 0), PLACES):
            total = total + parts[axis][((k >> shift) & 1) * 2 + ((j >> shift) & 1)]
        return total

    for block in range(HALF):
        row = pl.multiple_of(tile_of[owner(block)] * TILE, TILE)
        sem = sems.at[block // CHUNK]
        pltpu.make_async_copy(
            forward.at[0, :, pl.ds(row, TILE), :], fwd.at[block], sem
        ).start()
        pltpu.make_async_copy(
            adjoint.at[0, :, pl.ds(row, TILE), :], adj.at[block], sem
        ).start()
    freq = 1.0 + wl_index[0].astype(jnp.float32) / DEVICES
    square = freq * freq
    for chunk in range(HALF // CHUNK):
        these = pl.ds(chunk * CHUNK, CHUNK)
        for buffer in (fwd, adj):
            part = buffer.at[these]
            pltpu.make_async_copy(part, part, sems.at[chunk]).wait()
        for block in range(chunk * CHUNK, (chunk + 1) * CHUNK):
            out[block] = square * (
                fwd[block, 0] * adj[block, 0] - fwd[block, 1] * adj[block, 1]
            )


def weigh_kernel(foms, mine, other, out):
    me = flat_index()
    partner = me + CORE * (1 - 2 * lax.axis_index("c"))
    fom_sum = jnp.sum(foms[...], axis=0)[:, 0:1]
    scale = fom_sum / DEVICES + 1.0

    def weight(device):
        row = foms[device]
        return row[:, LANES // 2 : LANES // 2 + 1] - row[:, 0:1] / scale

    own, theirs = weight(me), weight(partner)
    for block in range(HALF):
        out[block] = own * mine[block] + theirs * other[block]


def shape_kernel(arrived, density, shaped, sent):
    total = arrived[0]
    for member in range(1, CUBE):
        total = total + arrived[member]
    bend = jnp.tanh(4.0 * (density[...] - 0.5))
    result = total * (4.0 * (1.0 - bend * bend))
    shaped[...] = result
    square = jnp.sum(result * result, axis=(0, 1), keepdims=True)
    sent[...] = jnp.broadcast_to(square[None], sent.shape)


def scale_kernel(squares, shaped, out):
    total = jnp.sum(squares[...], axis=0)[:, 0:1]
    norm = jnp.sqrt(total / (ROWS * COLS) + 1e-06)
    out[...] = shaped[...] / norm


def vmem():
    return pl.BlockSpec(memory_space=pltpu.VMEM)


def smem():
    return pl.BlockSpec(memory_space=pltpu.SMEM)


def hbm():
    return pl.BlockSpec(memory_space=pltpu.HBM)


def f32(*shape):
    return jax.ShapeDtypeStruct(shape, jnp.float32)


def grant(mib):
    return pltpu.CompilerParams(vmem_limit_bytes=mib * MIB)


def field(away, tile_of, wl_index, forward, adjoint):
    return pl.pallas_call(
        functools.partial(field_kernel, away),
        out_shape=f32(HALF, TILE, COLS),
        in_specs=[smem(), smem(), hbm(), hbm()],
        out_specs=vmem(),
        scratch_shapes=[
            pltpu.VMEM((HALF, 2, TILE, COLS), jnp.float32),
            pltpu.VMEM((HALF, 2, TILE, COLS), jnp.float32),
            pltpu.SemaphoreType.DMA((HALF // CHUNK,)),
        ],
        compiler_params=grant(16),
        name="field_away" if away else "field_own",
    )(tile_of, wl_index, forward, adjoint)


def exchanged(blocks, groups=None):
    return lax.all_to_all(blocks, AXES, 0, 0, tiled=True, axis_index_groups=groups)


def per_device(forward, adjoint, mode, target, wl_index, tile_of, density):
    fom_sent = pl.pallas_call(
        fom_kernel,
        out_shape=f32(DEVICES, 1, LANES),
        in_specs=[smem(), hbm(), vmem()],
        out_specs=vmem(),
        scratch_shapes=[
            pltpu.VMEM((2, TILE, COLS), jnp.float32),
            pltpu.SemaphoreType.DMA,
        ],
        compiler_params=grant(4),
        name="fom",
    )(target, forward, mode)
    foms = exchanged(fom_sent)
    away = field(True, tile_of, wl_index, forward, adjoint)
    other = lax.ppermute(away, "c", [(0, 1), (1, 0)])
    mine = field(False, tile_of, wl_index, forward, adjoint)
    weighted = pl.pallas_call(
        weigh_kernel,
        out_shape=f32(HALF, TILE, COLS),
        in_specs=[vmem(), vmem(), vmem()],
        out_specs=vmem(),
        compiler_params=grant(8),
        name="weigh",
    )(foms, mine, other)
    nearer = exchanged(weighted.reshape(CUBE, CUBE * TILE, COLS), cubes(FIRST)).sum(0)
    arrived = exchanged(nearer.reshape(CUBE, TILE, COLS), cubes(SECOND))
    shaped, square_sent = pl.pallas_call(
        shape_kernel,
        out_shape=[f32(TILE, COLS), f32(DEVICES, 1, LANES)],
        in_specs=[vmem(), vmem()],
        out_specs=[vmem(), vmem()],
        compiler_params=grant(4),
        name="shape",
    )(arrived, density)
    squares = exchanged(square_sent)
    return pl.pallas_call(
        scale_kernel,
        out_shape=f32(TILE, COLS),
        in_specs=[vmem(), vmem()],
        out_specs=vmem(),
        compiler_params=grant(4),
        name="scale",
    )(squares, shaped)


def solution(mesh):
    split = Mesh(mesh.devices.reshape(SIDE, SIDE, 2, SIDE), AXES)
    rows = P(AXES, None)
    placed = (
        P(AXES, None, None, None),
        P(AXES, None, None, None),
        P(),
        P(AXES),
        P(AXES),
        P(),
        rows,
    )
    return jax.shard_map(
        per_device, mesh=split, in_specs=placed, out_specs=rows, check_vma=False
    )
```

```python
import jax
import jax.numpy as jnp
from jax import lax
from jax.experimental import pallas as pl
from jax.experimental.pallas import tpu as pltpu
from jax.sharding import Mesh
from jax.sharding import PartitionSpec as P

AXES = ("x", "y", "c", "z")
PLACES = ("x", "y", "z")
SIDE = 4
DEVICES = 128
STRIDE = {"x": 32, "y": 8, "z": 1}
CORE = 4
ROWS = 1024
COLS = 1024
TILE = 8
CUBE = 8
HALF = DEVICES // 2
CHUNK = 8
LANES = 128
MIB = 1 << 20
FIELD_MIB = 20

EVEN = ((0, 1), (2, 3))
ODD = ((0, 3), (1, 2))
FIRST = (EVEN, ODD)
SECOND = (ODD, EVEN)


def cubes(pairs_of_core):
    groups = []
    for core, pairs in enumerate(pairs_of_core):
        for px in pairs:
            for py in pairs:
                for pz in pairs:
                    groups.append(
                        [
                            STRIDE["x"] * x + STRIDE["y"] * y + CORE * core + z
                            for x in px
                            for y in py
                            for z in pz
                        ]
                    )
    return groups


def pair_member(place, odd, bit):
    if odd:
        low = jnp.minimum(place, SIDE - 1 - place)
        return (SIDE - 1 - low) if bit else low
    return (place // 2) * 2 + bit


def owner_parts(core):
    parts = {}
    for axis in PLACES:
        place = lax.axis_index(axis)
        table = []
        for k in (0, 1):
            for j in (0, 1):
                even_first = pair_member(pair_member(place, False, k), True, j)
                odd_first = pair_member(pair_member(place, True, k), False, j)
                chosen = jnp.where(core == 0, even_first, odd_first)
                table.append(chosen * STRIDE[axis])
        parts[axis] = table
    return parts


def flat_index():
    place = CORE * lax.axis_index("c")
    for axis in PLACES:
        place = place + STRIDE[axis] * lax.axis_index(axis)
    return place


def gather_fields(away, tile_of, wl_index, forward, adjoint, out, fwd, adj, sems, between):
    core = lax.axis_index("c")
    keeper = (1 - core) if away else core
    parts = owner_parts(keeper)
    for block in range(HALF):
        k, j = divmod(block, CUBE)
        owner = CORE * keeper
        for shift, axis in zip((2, 1, 0), PLACES):
            bits = ((k >> shift) & 1) * 2 + ((j >> shift) & 1)
            owner = owner + parts[axis][bits]
        row = pl.multiple_of(tile_of[owner] * TILE, TILE)
        sem = sems.at[block // CHUNK]
        for source, buffer in ((forward, fwd), (adjoint, adj)):
            tile = source.at[0, :, pl.ds(row, TILE), :]
            pltpu.make_async_copy(tile, buffer.at[block], sem).start()
    between()
    freq = 1.0 + wl_index[0].astype(jnp.float32) / DEVICES
    square = freq * freq
    for chunk in range(HALF // CHUNK):
        these = pl.ds(chunk * CHUNK, CHUNK)
        for buffer in (fwd, adj):
            part = buffer.at[these]
            pltpu.make_async_copy(part, part, sems.at[chunk]).wait()
        for block in range(chunk * CHUNK, (chunk + 1) * CHUNK):
            out[block] = square * (
                fwd[block, 0] * adj[block, 0] - fwd[block, 1] * adj[block, 1]
            )


def away_kernel(
    tile_of,
    forward,
    adjoint,
    mode,
    wl_index_in,
    target_in,
    sent,
    out,
    fwd,
    adj,
    sems,
    line,
    wl_index,
    target,
    line_sem,
    scalar_sems,
):
    rows = forward.at[0, :, pl.ds(ROWS // 2, TILE), :]
    line_copy = pltpu.make_async_copy(rows, line, line_sem)
    wl_copy = pltpu.make_async_copy(wl_index_in, wl_index, scalar_sems.at[0])
    target_copy = pltpu.make_async_copy(target_in, target, scalar_sems.at[1])
    for copy in (line_copy, wl_copy, target_copy):
        copy.start()

    def send_fom():
        for copy in (line_copy, wl_copy, target_copy):
            copy.wait()
        re, im = line[0, 0:1, :], line[1, 0:1, :]
        mode_re, mode_im = mode[0:1, :], mode[1:2, :]
        over_re = jnp.sum(re * mode_re - im * mode_im, axis=1, keepdims=True)
        over_im = jnp.sum(re * mode_im + im * mode_re, axis=1, keepdims=True)
        fom = (over_re * over_re + over_im * over_im) / COLS
        lane = lax.broadcasted_iota(jnp.int32, (1, LANES), 1)
        row = jnp.where(lane < LANES // 2, fom, target[0])
        sent[...] = jnp.broadcast_to(row[None], sent.shape)

    gather_fields(
        True, tile_of, wl_index, forward, adjoint, out, fwd, adj, sems, send_fom
    )


def own_kernel(
    tile_of, forward, adjoint, wl_index_in, after, out, fwd, adj, sems, wl_index, sem
):
    wl_copy = pltpu.make_async_copy(wl_index_in, wl_index, sem)
    wl_copy.start()
    gather_fields(
        False, tile_of, wl_index, forward, adjoint, out, fwd, adj, sems, wl_copy.wait
    )


def weigh_kernel(foms, mine, other_hbm, out, other, sems):
    copies = []
    for chunk in range(HALF // CHUNK):
        these = pl.ds(chunk * CHUNK, CHUNK)
        copy = pltpu.make_async_copy(other_hbm.at[these], other.at[these], sems.at[chunk])
        copy.start()
        copies.append(copy)
    me = flat_index()
    partner = me + CORE * (1 - 2 * lax.axis_index("c"))
    fom_sum = jnp.sum(foms[...], axis=0)[:, 0:1]
    scale = fom_sum / DEVICES + 1.0

    def weight(device):
        row = foms[device]
        return row[:, LANES // 2 : LANES // 2 + 1] - row[:, 0:1] / scale

    own, theirs = weight(me), weight(partner)
    for block in range(HALF):
        if block % CHUNK == 0:
            copies[block // CHUNK].wait()
        out[block] = own * mine[block] + theirs * other[block]


def shape_kernel(arrived, density, shaped, sent):
    total = arrived[0]
    for member in range(1, CUBE):
        total = total + arrived[member]
    bend = jnp.tanh(4.0 * (density[...] - 0.5))
    result = total * (4.0 * (1.0 - bend * bend))
    shaped[...] = result
    square = jnp.sum(result * result, axis=(0, 1), keepdims=True)
    sent[...] = jnp.broadcast_to(square[None], sent.shape)


def scale_kernel(squares, shaped, out):
    total = jnp.sum(squares[...], axis=0)[:, 0:1]
    norm = jnp.sqrt(total / (ROWS * COLS) + 1e-06)
    out[...] = shaped[...] / norm


def vmem():
    return pl.BlockSpec(memory_space=pltpu.VMEM)


def smem():
    return pl.BlockSpec(memory_space=pltpu.SMEM)


def hbm():
    return pl.BlockSpec(memory_space=pltpu.HBM)


def f32(*shape):
    return jax.ShapeDtypeStruct(shape, jnp.float32)


def vmem_f32(*shape):
    return pltpu.VMEM(shape, jnp.float32)


def in_hbm(array):
    return pltpu.with_memory_space_constraint(array, pltpu.HBM)


def grant(mib):
    return pltpu.CompilerParams(vmem_limit_bytes=mib * MIB)


def exchanged(blocks, groups=None):
    return lax.all_to_all(blocks, AXES, 0, 0, tiled=True, axis_index_groups=groups)


def per_device(forward, adjoint, mode, target, wl_index, tile_of, density):
    forward, adjoint, mode, tile_of = (
        in_hbm(array) for array in (forward, adjoint, mode, tile_of)
    )
    buffer = pltpu.VMEM((HALF, 2, TILE, COLS), jnp.float32)
    gather_scratch = [buffer, buffer, pltpu.SemaphoreType.DMA((HALF // CHUNK,))]
    fom_sent, away = pl.pallas_call(
        away_kernel,
        out_shape=[vmem_f32(DEVICES, 1, LANES), vmem_f32(HALF, TILE, COLS)],
        in_specs=[smem(), hbm(), hbm(), vmem(), hbm(), hbm()],
        out_specs=[vmem(), vmem()],
        scratch_shapes=[
            *gather_scratch,
            pltpu.VMEM((2, TILE, COLS), jnp.float32),
            pltpu.SMEM((1,), jnp.int32),
            pltpu.SMEM((1,), jnp.float32),
            pltpu.SemaphoreType.DMA,
            pltpu.SemaphoreType.DMA((2,)),
        ],
        compiler_params=grant(FIELD_MIB),
        name="field_away",
    )(tile_of, forward, adjoint, mode, wl_index, target)
    other = lax.ppermute(away, "c", [(0, 1), (1, 0)])
    foms = exchanged(fom_sent)
    mine = pl.pallas_call(
        own_kernel,
        out_shape=vmem_f32(HALF, TILE, COLS),
        in_specs=[smem(), hbm(), hbm(), hbm(), hbm()],
        out_specs=vmem(),
        scratch_shapes=[
            *gather_scratch,
            pltpu.SMEM((1,), jnp.int32),
            pltpu.SemaphoreType.DMA,
        ],
        compiler_params=grant(FIELD_MIB),
        name="field_own",
    )(tile_of, forward, adjoint, wl_index, fom_sent)
    weighted = pl.pallas_call(
        weigh_kernel,
        out_shape=vmem_f32(HALF, TILE, COLS),
        in_specs=[vmem(), vmem(), hbm()],
        out_specs=vmem(),
        scratch_shapes=[
            pltpu.VMEM((HALF, TILE, COLS), jnp.float32),
            pltpu.SemaphoreType.DMA((HALF // CHUNK,)),
        ],
        compiler_params=grant(8),
        name="weigh",
    )(foms, mine, in_hbm(other))
    nearer = exchanged(weighted.reshape(CUBE, CUBE * TILE, COLS), cubes(FIRST)).sum(0)
    arrived = exchanged(nearer.reshape(CUBE, TILE, COLS), cubes(SECOND))
    shaped, square_sent = pl.pallas_call(
        shape_kernel,
        out_shape=[f32(TILE, COLS), f32(DEVICES, 1, LANES)],
        in_specs=[vmem(), vmem()],
        out_specs=[vmem(), vmem()],
        compiler_params=grant(4),
        name="shape",
    )(arrived, density)
    squares = exchanged(square_sent)
    return pl.pallas_call(
        scale_kernel,
        out_shape=f32(TILE, COLS),
        in_specs=[vmem(), vmem()],
        out_specs=vmem(),
        compiler_params=grant(4),
        name="scale",
    )(squares, shaped)


def solution(mesh):
    split = Mesh(mesh.devices.reshape(SIDE, SIDE, 2, SIDE), AXES)
    rows = P(AXES, None)
    placed = (
        P(AXES, None, None, None),
        P(AXES, None, None, None),
        P(),
        P(AXES),
        P(AXES),
        P(),
        rows,
    )
    return jax.shard_map(
        per_device, mesh=split, in_specs=placed, out_specs=rows, check_vma=False
    )
```

```python
import jax
import jax.numpy as jnp
from jax import lax
from jax.experimental import pallas as pl
from jax.experimental.pallas import tpu as pltpu
from jax.sharding import Mesh
from jax.sharding import PartitionSpec as P

AXES = ("x", "y", "c", "z")
PLACES = ("x", "y", "z")
SIDE = 4
DEVICES = 128
STRIDE = {"x": 32, "y": 8, "z": 1}
CORE = 4
ROWS = 1024
COLS = 1024
TILE = 8
CUBE = 8
HALF = DEVICES // 2
CHUNK = 4
LANES = 128
MIB = 1 << 20
FIELD_MIB = 20

EVEN = ((0, 1), (2, 3))
ODD = ((0, 3), (1, 2))
FIRST = (EVEN, ODD)
SECOND = (ODD, EVEN)


def cubes(pairs_of_core):
    groups = []
    for core, pairs in enumerate(pairs_of_core):
        for px in pairs:
            for py in pairs:
                for pz in pairs:
                    groups.append(
                        [
                            STRIDE["x"] * x + STRIDE["y"] * y + CORE * core + z
                            for x in px
                            for y in py
                            for z in pz
                        ]
                    )
    return groups


def pair_member(place, odd, bit):
    if odd:
        low = jnp.minimum(place, SIDE - 1 - place)
        return (SIDE - 1 - low) if bit else low
    return (place // 2) * 2 + bit


def owner_parts(core):
    parts = {}
    for axis in PLACES:
        place = lax.axis_index(axis)
        table = []
        for k in (0, 1):
            for j in (0, 1):
                even_first = pair_member(pair_member(place, False, k), True, j)
                odd_first = pair_member(pair_member(place, True, k), False, j)
                chosen = jnp.where(core == 0, even_first, odd_first)
                table.append(chosen * STRIDE[axis])
        parts[axis] = table
    return parts


def flat_index():
    place = CORE * lax.axis_index("c")
    for axis in PLACES:
        place = place + STRIDE[axis] * lax.axis_index(axis)
    return place


def gather_fields(away, tile_of, wl_index, forward, adjoint, out, fwd, adj, sems, between):
    core = lax.axis_index("c")
    keeper = (1 - core) if away else core
    parts = owner_parts(keeper)
    for block in range(HALF):
        k, j = divmod(block, CUBE)
        owner = CORE * keeper
        for shift, axis in zip((2, 1, 0), PLACES):
            bits = ((k >> shift) & 1) * 2 + ((j >> shift) & 1)
            owner = owner + parts[axis][bits]
        row = pl.multiple_of(tile_of[owner] * TILE, TILE)
        sem = sems.at[block // CHUNK]
        for source, buffer in ((forward, fwd), (adjoint, adj)):
            tile = source.at[0, :, pl.ds(row, TILE), :]
            pltpu.make_async_copy(tile, buffer.at[block], sem).start()
    between()
    freq = 1.0 + wl_index[0].astype(jnp.float32) / DEVICES
    square = freq * freq
    for chunk in range(HALF // CHUNK):
        these = pl.ds(chunk * CHUNK, CHUNK)
        for buffer in (fwd, adj):
            part = buffer.at[these]
            pltpu.make_async_copy(part, part, sems.at[chunk]).wait()
        for block in range(chunk * CHUNK, (chunk + 1) * CHUNK):
            out[block] = square * (
                fwd[block, 0] * adj[block, 0] - fwd[block, 1] * adj[block, 1]
            )


def away_kernel(
    tile_of,
    forward,
    adjoint,
    mode_hbm,
    wl_index,
    target,
    sent,
    out,
    fwd,
    adj,
    sems,
    line,
    line_sem,
    mode,
    mode_sem,
):
    rows = forward.at[0, :, pl.ds(ROWS // 2, TILE), :]
    line_copy = pltpu.make_async_copy(rows, line, line_sem)
    mode_copy = pltpu.make_async_copy(mode_hbm, mode, mode_sem)
    small = (line_copy, mode_copy)
    for copy in small:
        copy.start()

    def send_fom():
        for copy in small:
            copy.wait()
        re, im = line[0, 0:1, :], line[1, 0:1, :]
        mode_re, mode_im = mode[0:1, :], mode[1:2, :]
        over_re = jnp.sum(re * mode_re - im * mode_im, axis=1, keepdims=True)
        over_im = jnp.sum(re * mode_im + im * mode_re, axis=1, keepdims=True)
        fom = (over_re * over_re + over_im * over_im) / COLS
        lane = lax.broadcasted_iota(jnp.int32, (1, LANES), 1)
        row = jnp.where(lane < LANES // 2, fom, target[0])
        sent[...] = jnp.broadcast_to(row[None], sent.shape)

    gather_fields(
        True, tile_of, wl_index, forward, adjoint, out, fwd, adj, sems, send_fom
    )


def own_kernel(
    tile_of, forward, adjoint, wl_index, after, out, fwd, adj, sems
):
    gather_fields(
        False, tile_of, wl_index, forward, adjoint, out, fwd, adj, sems, lambda: None
    )


def weigh_kernel(foms, mine, other_hbm, out, other, sems):
    copies = []
    for chunk in range(HALF // CHUNK):
        these = pl.ds(chunk * CHUNK, CHUNK)
        copy = pltpu.make_async_copy(other_hbm.at[these], other.at[these], sems.at[chunk])
        copy.start()
        copies.append(copy)
    me = flat_index()
    partner = me + CORE * (1 - 2 * lax.axis_index("c"))
    fom_sum = jnp.sum(foms[...], axis=0)[:, 0:1]
    scale = fom_sum / DEVICES + 1.0

    def weight(device):
        row = foms[device]
        return row[:, LANES // 2 : LANES // 2 + 1] - row[:, 0:1] / scale

    own, theirs = weight(me), weight(partner)
    for block in range(HALF):
        if block % CHUNK == 0:
            copies[block // CHUNK].wait()
        out[block] = own * mine[block] + theirs * other[block]


def shape_kernel(arrived, density, shaped, sent):
    total = arrived[0]
    for member in range(1, CUBE):
        total = total + arrived[member]
    bend = jnp.tanh(4.0 * (density[...] - 0.5))
    result = total * (4.0 * (1.0 - bend * bend))
    shaped[...] = result
    square = jnp.sum(result * result, axis=(0, 1), keepdims=True)
    sent[...] = jnp.broadcast_to(square[None], sent.shape)


def scale_kernel(squares, shaped, out):
    total = jnp.sum(squares[...], axis=0)[:, 0:1]
    norm = jnp.sqrt(total / (ROWS * COLS) + 1e-06)
    out[...] = shaped[...] / norm


def vmem():
    return pl.BlockSpec(memory_space=pltpu.VMEM)


def smem():
    return pl.BlockSpec(memory_space=pltpu.SMEM)


def hbm():
    return pl.BlockSpec(memory_space=pltpu.HBM)


def f32(*shape):
    return jax.ShapeDtypeStruct(shape, jnp.float32)


def vmem_f32(*shape):
    return pltpu.VMEM(shape, jnp.float32)


def in_hbm(array):
    return pltpu.with_memory_space_constraint(array, pltpu.HBM)


def grant(mib):
    return pltpu.CompilerParams(vmem_limit_bytes=mib * MIB)


def exchanged(blocks, groups=None):
    return lax.all_to_all(blocks, AXES, 0, 0, tiled=True, axis_index_groups=groups)


def per_device(forward, adjoint, mode, target, wl_index, tile_of, density):
    forward, adjoint, mode, tile_of = (
        in_hbm(array) for array in (forward, adjoint, mode, tile_of)
    )
    buffer = pltpu.VMEM((HALF, 2, TILE, COLS), jnp.float32)
    gather_scratch = [buffer, buffer, pltpu.SemaphoreType.DMA((HALF // CHUNK,))]
    fom_sent, away = pl.pallas_call(
        away_kernel,
        out_shape=[vmem_f32(DEVICES, 1, LANES), vmem_f32(HALF, TILE, COLS)],
        in_specs=[smem(), hbm(), hbm(), hbm(), smem(), smem()],
        out_specs=[vmem(), vmem()],
        scratch_shapes=[
            *gather_scratch,
            pltpu.VMEM((2, TILE, COLS), jnp.float32),
            pltpu.SemaphoreType.DMA,
            pltpu.VMEM((2, COLS), jnp.float32),
            pltpu.SemaphoreType.DMA,
        ],
        compiler_params=grant(FIELD_MIB),
        name="field_away",
    )(tile_of, forward, adjoint, mode, wl_index, target)
    other = lax.ppermute(away, "c", [(0, 1), (1, 0)])
    foms = exchanged(fom_sent)
    mine = pl.pallas_call(
        own_kernel,
        out_shape=vmem_f32(HALF, TILE, COLS),
        in_specs=[smem(), hbm(), hbm(), smem(), hbm()],
        out_specs=vmem(),
        scratch_shapes=gather_scratch,
        compiler_params=grant(FIELD_MIB),
        name="field_own",
    )(tile_of, forward, adjoint, wl_index, fom_sent)
    weighted = pl.pallas_call(
        weigh_kernel,
        out_shape=vmem_f32(HALF, TILE, COLS),
        in_specs=[vmem(), vmem(), hbm()],
        out_specs=vmem(),
        scratch_shapes=[
            pltpu.VMEM((HALF, TILE, COLS), jnp.float32),
            pltpu.SemaphoreType.DMA((HALF // CHUNK,)),
        ],
        compiler_params=grant(8),
        name="weigh",
    )(foms, mine, in_hbm(other))
    nearer = exchanged(weighted.reshape(CUBE, CUBE * TILE, COLS), cubes(FIRST)).sum(0)
    arrived = exchanged(nearer.reshape(CUBE, TILE, COLS), cubes(SECOND))
    shaped, square_sent = pl.pallas_call(
        shape_kernel,
        out_shape=[f32(TILE, COLS), f32(DEVICES, 1, LANES)],
        in_specs=[vmem(), vmem()],
        out_specs=[vmem(), vmem()],
        compiler_params=grant(4),
        name="shape",
    )(arrived, density)
    squares = exchanged(square_sent)
    return pl.pallas_call(
        scale_kernel,
        out_shape=f32(TILE, COLS),
        in_specs=[vmem(), vmem()],
        out_specs=vmem(),
        compiler_params=grant(4),
        name="scale",
    )(squares, shaped)


def solution(mesh):
    split = Mesh(mesh.devices.reshape(SIDE, SIDE, 2, SIDE), AXES)
    rows = P(AXES, None)
    placed = (
        P(AXES, None, None, None),
        P(AXES, None, None, None),
        P(),
        P(AXES),
        P(AXES),
        P(),
        rows,
    )
    return jax.shard_map(
        per_device, mesh=split, in_specs=placed, out_specs=rows, check_vma=False
    )
```
